32 devices in a mesh: dp: 8 (over z, x), expert: 4 (over y, core).
Axes of the slice: x: 2, y: 2, z: 4, core: 2. Of those that a mesh axis runs over, the one named last changes fastest.
Arguments:
- inputs: bfloat16 [18912, 768], P(('dp', 'expert')), may hold values from -24 to 24, as said below
- cotangent: bfloat16 [18912, 768], P(('dp', 'expert')), may hold values from -6 to 6
- routes: int32 [2, 18912, 2], P(None, ('dp', 'expert')), may hold values from 0 to 3, all different within a row; in each aligned block of 591 rows (0 to 590, 591 to 1181, ..., all dimensions but the last counted through in order) at most 369 rows name the same one
- keep: int32 [2, 18912, 2], P(None, ('dp', 'expert')), may hold values from 0 to 1
- norm_gain: float32 [2, 768, 2], replicated, may hold values from 0.25 to 1.75
- norm_bias: float32 [2, 768, 2], replicated, may hold values from -3 to 3
- qkv_weight: bfloat16 [2, 768, 2304], replicated, may hold values from -0.21875 to 0.21875
- out_weight: bfloat16 [2, 768, 768], replicated, may hold values from -0.625 to 0.625
- router_weight: bfloat16 [2, 768, 4], replicated, may hold values from -0.3125 to 0.3125
- up_weight: bfloat16 [2, 4, 768, 3072], P(None, 'expert'), may hold values from -0.21875 to 0.21875
- down_weight: bfloat16 [2, 4, 3072, 768], P(None, 'expert'), may hold values from -0.625 to 0.625
Outputs:
- activations: bfloat16 [18912, 768], P(('dp', 'expert'))
- aux_loss: float32 [], replicated
- input_grad: float32 [18912, 768], P(('dp', 'expert'))
- gain_grad: float32 [2, 768, 2], P(None, 'dp')
- bias_grad: float32 [2, 768, 2], P(None, 'dp')
- qkv_grad: float32 [2, 768, 2304], P(None, 'dp')
- out_grad: float32 [2, 768, 768], P(None, 'dp')
- router_grad: float32 [2, 768, 4], P(None, 'dp')
- up_grad: float32 [2, 4, 768, 3072], P(None, 'expert', 'dp')
- down_grad: float32 [2, 4, 3072, 768], P(None, 'expert', 'dp')
The draws below stay inside these ranges and needn't reach their ends.
Inputs may be any that keep to these rules, and one draw needn't show every extreme that they name: `inputs`: activations whose mean direction drifts across the token order. `routes`: each token names two different experts in each block. Among the 591 rows of one device in one block, no expert is named more than 369 times, a bound that some block reaches.
All inputs are finite; a program needn't handle non-finite values.
Results may differ from the reference program's by a relative error of at most 0.025.
Values may be sent and summed in bfloat16 or wider, within the bound.
No kernel may reach another device: no remote copies, remote signals or barrier semaphores. Data moves between devices by JAX's collectives and lax.ppermute only.
A program may use at most 320 MiB of HBM per device.

```python
import math
import jax
import jax.numpy as jnp
import numpy as np
from jax import lax

D = 768
HEADS = 12
HEAD_DIM = 64
HID = 3072
SEQ = 197
LAYERS = 2
IMG_DEV = 3
EXPERTS = 4
TOK_DEV = 591
TOKENS = 18912
CAP = 369
DEVICES = 32


def draw_inputs(key, part):
    noise_key = jax.random.fold_in(key, 11)
    line_key = jax.random.fold_in(key, 12)
    base = jnp.clip(jax.random.normal(noise_key, (TOKENS, D), jnp.float32), -6.0, 6.0)
    line = jnp.clip(jax.random.normal(line_key, (D,), jnp.float32), -4.0, 4.0)
    ramp = 2.0 * jnp.arange(TOKENS, dtype=jnp.float32) / TOKENS
    return (base + ramp[:, None] * line[None, :]).astype(jnp.bfloat16)


def draw_keep(key, part):
    rolls = jax.random.randint(jax.random.fold_in(key, 21), (LAYERS, TOKENS, 2), 0, 1000, dtype=jnp.int32)
    position = jnp.arange(TOKENS, dtype=jnp.int32)
    limit = 300 + 650 * position // TOKENS
    return (rolls < limit[None, :, None]).astype(jnp.int32)


def block_levels(own_key, extent, pieces, low, top_value):
    loudness, own = 1.0, jax.random.fold_in(own_key, 6)
    for dim, parts in pieces:
        steps = jnp.exp(jax.random.uniform(jax.random.fold_in(own, dim), (parts,), jnp.float32, low / len(pieces), top_value / len(pieces)))
        loudness = loudness * jnp.repeat(steps, extent[dim] // parts).reshape([-1 if axis == dim else 1 for axis in range(len(extent))])
    return loudness


def deal_out(rng, own, number, rows, amount, top, reach, slope):
    order = jax.random.permutation(rng, amount)
    crowded, usual = portions_of(amount, rows * top, reach, slope, True), portions_of(amount, rows * top, reach, slope, False)
    places = jnp.arange(amount)

    def named(sizes, turn):
        used = int((sizes > 0).sum())
        fixed = max(1, used // 4)
        passed = fixed + (places - fixed + turn * (used - fixed)) % max(1, amount - fixed)
        return jnp.zeros((amount,), jnp.int32).at[order[jnp.where(places < fixed, places, passed)]].set(jnp.asarray(sizes, jnp.int32))

    sizes = jnp.where(number % 4 == 0, named(crowded, number // 4), named(usual, number - number // 4 - 1))
    mixed = jax.random.permutation(jax.random.fold_in(own, 3), amount)
    donor, taker = mixed[0:amount // 2 * 2:2], mixed[1:amount // 2 * 2:2]
    slack = jnp.minimum(sizes[donor] - 1, reach - sizes[taker]) // 2
    slack = jnp.where((donor == order[0]) | (taker == order[0]) | (sizes[taker] == 0), 0, jnp.maximum(slack, 0))
    passed = jax.random.randint(jax.random.fold_in(own, 4), (amount // 2,), 0, 1 << 20) % (slack + 1)
    sizes = sizes.at[donor].add(-passed).at[taker].add(passed)
    labels = jnp.searchsorted(jnp.cumsum(sizes), jnp.arange(rows * top), side="right").astype(jnp.int32)
    grid = labels.reshape(top, rows).T
    grid = grid[jax.random.permutation(jax.random.fold_in(own, 1), rows)]
    turn = jax.random.randint(jax.random.fold_in(own, 2), (rows, 1), 0, top)
    return jnp.take_along_axis(grid, (jnp.arange(top)[None, :] + turn) % top, axis=1)


def portions_of(amount, total, reach, slope, full):
    weights = [(1 << 20) // math.isqrt(standing ** slope) + 1 for standing in range(1, amount + 1)]
    largest = reach if full else min(reach, max(-(-total // amount), total * weights[0] // sum(weights)))
    least = 1 if total - largest >= amount - 1 else 0
    given, rest = [largest] + [least] * (amount - 1), total - largest - least * (amount - 1)
    while rest > 0:
        movable = [i for i in range(1, amount) if given[i] < largest] or [i for i in range(1, amount) if given[i] < reach]
        pool, budget = sum([weights[i] for i in movable]), rest
        for i in movable:
            more = min(reach - given[i], max(1, budget * weights[i] // pool), rest)
            given[i] = given[i] + more
            rest = rest - more
    return np.array(given)


def normal_values(key, extent, scale, bound, split=(), held_as=jnp.bfloat16):
    level = block_levels(key, extent, split, -0.22, 0.18) if split else 1.0
    result = jax.random.normal(key, extent, jnp.float32) * scale * level
    return jnp.minimum(jnp.maximum(result, -bound), bound).astype(held_as)


def setup_inputs(seed: int = 0) -> dict:
    streams_of = jax.random.split(jax.random.key(seed), 12)
    inputs = draw_inputs(jax.random.fold_in(streams_of[11], 71), 0)
    cotangent = normal_values(streams_of[1], (TOKENS, D), 1.0, 6.0, ((0, 32),))
    routes_keys = jax.random.split(jax.random.fold_in(streams_of[2], 1), LAYERS * TOKENS // TOK_DEV)
    routes_turns = jax.random.permutation(jax.random.fold_in(streams_of[2], 3), LAYERS * TOKENS // TOK_DEV)
    routes = jax.vmap(lambda own, number: deal_out(jax.random.fold_in(streams_of[2], 2), own, number, TOK_DEV, EXPERTS, 2, CAP, 1))(routes_keys, routes_turns).reshape((LAYERS, TOKENS, 2))
    keep = draw_keep(jax.random.fold_in(streams_of[11], 71), 0)
    norm_gain = jnp.clip(1.0 + 0.15 * jax.random.normal(streams_of[4], (LAYERS, D, 2), jnp.float32), 0.25, 1.75)
    norm_bias = normal_values(streams_of[5], (LAYERS, D, 2), 0.5, 3.0, (), jnp.float32)
    qkv_weight = normal_values(streams_of[6], (LAYERS, D, 3 * D), D ** -0.5, 0.21875)
    out_weight = normal_values(streams_of[7], (LAYERS, D, D), (D // 8) ** -0.5, 0.625)
    router_weight = normal_values(streams_of[8], (LAYERS, D, EXPERTS), (D // 2) ** -0.5, 0.3125)
    up_weight = normal_values(streams_of[9], (LAYERS, EXPERTS, D, HID), D ** -0.5, 0.21875, ((1, 4),))
    down_weight = normal_values(streams_of[10], (LAYERS, EXPERTS, HID, D), (HID // 32) ** -0.5, 0.625, ((1, 4),))
    return {"inputs": inputs, "cotangent": cotangent, "routes": routes, "keep": keep, "norm_gain": norm_gain, "norm_bias": norm_bias, "qkv_weight": qkv_weight, "out_weight": out_weight, "router_weight": router_weight, "up_weight": up_weight, "down_weight": down_weight}


EPS = 1e-06
BALANCE_WEIGHT = 0.01
HIGHEST_MODE = lax.Precision.HIGHEST

@jax.custom_vjp
def low(v):
    return lax.optimization_barrier(v.astype(jnp.bfloat16)).astype(jnp.float32)

@jax.custom_vjp
def low_back(v):
    return v

def low_keep(v):
    return (low(v), None)

def low_pass(kept, grad):
    return (grad,)

def back_keep(v):
    return (v, None)

def back_low(kept, grad):
    return (low(grad),)
low.defvjp(low_keep, low_pass)
low_back.defvjp(back_keep, back_low)

def product(left, right):
    return jnp.dot(left, right, precision=HIGHEST_MODE)

def normalize(features, gain_row, bias_row):
    row_mean = lax.optimization_barrier(jnp.mean(features, axis=-1, keepdims=True))
    centred = features - row_mean
    spread = lax.optimization_barrier(jnp.mean(centred * centred, axis=-1, keepdims=True))
    return centred * lax.rsqrt(spread + EPS) * gain_row + bias_row

def attention_block(projected):
    shaped = projected.reshape(IMG_DEV, SEQ, 3, HEADS, HEAD_DIM)
    queries = shaped[:, :, 0]
    key_rows = shaped[:, :, 1]
    values = shaped[:, :, 2]
    scores = low_back(HEAD_DIM ** (-0.5) * jnp.einsum('bqhd,bkhd->bhqk', queries, key_rows, precision=HIGHEST_MODE))
    weights = low(jax.nn.softmax(scores, axis=-1))
    attended = jnp.einsum('bhqk,bkhd->bqhd', weights, values, precision=HIGHEST_MODE)
    return attended.reshape(TOK_DEV, D)

def expert_block(operands):
    expert_rows, up_matrix, down_matrix = operands
    pre_gelu = low_back(product(expert_rows, up_matrix))
    hidden = low(jax.nn.gelu(pre_gelu, approximate=False))
    return product(hidden, down_matrix)

def slot_table(chosen):
    onehot = (chosen[:, None] == jnp.arange(EXPERTS, dtype=jnp.int32)[None, :]).astype(jnp.int32)
    before = jnp.cumsum(onehot, axis=0, dtype=jnp.int32) - onehot
    return lax.optimization_barrier(jnp.sum(before * onehot, axis=1, dtype=jnp.int32))

def place(payload, target):
    return jnp.zeros((EXPERTS * CAP, D), jnp.float32).at[target].set(payload)

def pick(table, target):
    return table[target]

def reference(inputs, cotangent, routes, keep, norm_gain, norm_bias, qkv_weight, out_weight, router_weight, up_weight, down_weight):
    keep_float = keep.astype(jnp.float32)
    flat_routes = routes.reshape(LAYERS, DEVICES, 2 * TOK_DEV).astype(jnp.int32)
    targets = (flat_routes * CAP + jax.vmap(jax.vmap(slot_table))(flat_routes)).astype(jnp.int32)
    pair_hot = (routes[..., None] == jnp.arange(EXPERTS, dtype=jnp.int32)).astype(jnp.float32)
    counts = lax.optimization_barrier(jnp.sum(pair_hot * keep_float[..., None], axis=(1, 2)))

    def forward(residual, gains, biases, w_qkv, w_out, w_route, w_up, w_down):
        aux_loss = jnp.zeros((), jnp.float32)
        for depth_index in range(LAYERS):
            normed_first = low(normalize(residual, gains[depth_index, :, 0], biases[depth_index, :, 0]))
            projected = low(low_back(product(normed_first, w_qkv[depth_index])))
            attended = lax.map(jax.checkpoint(attention_block), projected.reshape(DEVICES, TOK_DEV, 3 * D))
            attended = low(low_back(attended.reshape(TOKENS, D)))
            middle = residual + low_back(product(attended, w_out[depth_index]))
            second = low(normalize(middle, gains[depth_index, :, 1], biases[depth_index, :, 1]))
            router_probs = jax.nn.softmax(product(second, w_route[depth_index]), axis=-1)
            gate_values = keep_float[depth_index] * lax.optimization_barrier(jnp.sum(pair_hot[depth_index] * router_probs[:, None, :], axis=-1))
            aux_loss = aux_loss + EXPERTS * jnp.sum(counts[depth_index] / (2 * TOKENS) * lax.optimization_barrier(jnp.mean(router_probs, axis=0)))
            payload = (second[:, None, :] * keep_float[depth_index][:, :, None]).reshape(DEVICES, 2 * TOK_DEV, D)
            buffers = jax.vmap(place)(payload, targets[depth_index])
            expert_rows = buffers.reshape(DEVICES, EXPERTS, CAP, D).transpose(1, 0, 2, 3).reshape(EXPERTS, DEVICES * CAP, D)
            expert_rows = low_back(expert_rows)
            produced = lax.map(jax.checkpoint(expert_block), (expert_rows, w_up[depth_index], w_down[depth_index]))
            produced = low(low_back(produced))
            returned = produced.reshape(EXPERTS, DEVICES, CAP, D).transpose(1, 0, 2, 3).reshape(DEVICES, EXPERTS * CAP, D)
            picked = jax.vmap(pick)(returned, targets[depth_index]).reshape(TOKENS, 2, D)
            residual = middle + lax.optimization_barrier(jnp.sum(gate_values[:, :, None] * picked, axis=1))
        return (residual, aux_loss)
    (final, aux_loss), pull = jax.vjp(forward, inputs.astype(jnp.float32), norm_gain.astype(jnp.float32), norm_bias.astype(jnp.float32), qkv_weight.astype(jnp.float32), out_weight.astype(jnp.float32), router_weight.astype(jnp.float32), up_weight.astype(jnp.float32), down_weight.astype(jnp.float32))
    grads = pull((cotangent.astype(jnp.float32), jnp.asarray(BALANCE_WEIGHT, jnp.float32)))
    return (final.astype(jnp.bfloat16), aux_loss, grads[0], grads[1], grads[2], grads[3], grads[4], grads[5], grads[6], grads[7])
```

```python
import functools

import jax
import jax.numpy as jnp
from jax import lax
from jax.experimental import pallas as pl
from jax.experimental.pallas import tpu as pltpu
from jax.sharding import PartitionSpec as P

HEADS = 12
HEAD_DIM = 64
SEQ = 197
PAD = 208
SIDE = 200
EPS = 1e-06
BALANCE_WEIGHT = 0.01
TILE = 256
CHUNKS = (1, 1, 1)
BF = jnp.bfloat16
F32 = jnp.float32
NT = (((1,), (1,)), ((), ()))
TN = (((0,), (0,)), ((), ()))
VMEM_LIMIT = 60 * 1024 * 1024


def dot(a, b, dims=(((1,), (0,)), ((), ()))):
    return lax.dot_general(a, b, dims, preferred_element_type=F32)


def iota(shape, axis):
    return lax.broadcasted_iota(jnp.int32, shape, axis)


def params():
    return pltpu.CompilerParams(
        dimension_semantics=("arbitrary",), vmem_limit_bytes=VMEM_LIMIT
    )


def cost(flops, size):
    return pl.CostEstimate(flops=int(flops), bytes_accessed=int(size), transcendentals=0)


def sds(shape, dtype):
    return jax.ShapeDtypeStruct(shape, dtype)


def whole(shape):
    return pl.BlockSpec(shape, lambda i: (0,) * len(shape))


def row_stats(v):
    width = v.shape[-1]
    mean = jnp.sum(v, axis=-1, keepdims=True) * (1.0 / width)
    centred = v - mean
    spread = jnp.sum(centred * centred, axis=-1, keepdims=True) * (1.0 / width)
    scale = lax.rsqrt(spread + EPS)
    return centred * scale, scale


def norm_back(u, gain, rows, scale):
    width = u.shape[-1]
    ug = u * gain
    first = jnp.sum(ug, axis=-1, keepdims=True) * (1.0 / width)
    second = jnp.sum(ug * rows, axis=-1, keepdims=True) * (1.0 / width)
    return scale * (ug - first - rows * second)


def router_rows(router, rows, experts):
    logits = dot(router, rows, NT)
    named = iota(logits.shape, 0) < experts
    logits = jnp.where(named, logits, -1e30)
    top = jnp.max(logits, axis=0, keepdims=True)
    raised = jnp.where(named, jnp.exp(logits - top), 0.0)
    return raised / jnp.sum(raised, axis=0, keepdims=True)


def halves(block):
    low = iota(block.shape, 1) < HEAD_DIM
    zero = jnp.zeros_like(block)
    return jnp.where(low, block, zero), jnp.where(low, zero, block)


def attention_forward_kernel(first, parts, *refs):
    ins = refs[: parts + 5]
    outs = refs[parts + 5 :]
    norms, qkv_w, out_w = ins[parts : parts + 3]
    del ins
    total = refs[0][...].astype(F32)
    for ref in refs[1:parts]:
        total = total + ref[...].astype(F32)
    outs = refs[parts + 3 :]
    if not first:
        outs[-1][...] = total
    normed_o, qkv_o, att_o, lse_o, middle_o, second_o = outs[:6]
    rows, _ = row_stats(total)
    normed = (rows * norms[0, 0:1, :] + norms[0, 1:2, :]).astype(BF)
    normed_o[...] = normed
    qkv_o[...] = dot(normed, qkv_w[0]).astype(BF)
    width = total.shape[1]
    keys_ok = iota((PAD, PAD), 1) < SEQ
    lane = iota((PAD, 128), 1)
    lse = jnp.zeros((PAD, 128), F32)
    for pair in range(width // 128):
        cols = slice(pair * 128, pair * 128 + 128)
        query = qkv_o[:, cols]
        key = qkv_o[:, width + pair * 128 : width + pair * 128 + 128]
        value = qkv_o[:, 2 * width + pair * 128 : 2 * width + pair * 128 + 128]
        mixed = jnp.zeros((PAD, 128), F32)
        for side, (q_half, v_half) in enumerate(zip(halves(query), halves(value))):
            scores = dot(q_half, key, NT) * (HEAD_DIM ** (-0.5))
            scores = jnp.where(keys_ok, scores, -1e30)
            top = jnp.max(scores, axis=1, keepdims=True)
            raised = jnp.exp(scores - top)
            total_r = jnp.sum(raised, axis=1, keepdims=True)
            weights = (raised * (1.0 / total_r)).astype(BF)
            mixed = mixed + dot(weights, v_half)
            lse = jnp.where(lane == 2 * pair + side, top + jnp.log(total_r), lse)
        att_o[:, cols] = mixed.astype(BF)
    lse_o[...] = lse
    middle = total + dot(att_o[...], out_w[0])
    middle_o[...] = middle
    rows, _ = row_stats(middle)
    second_o[...] = (rows * norms[0, 2:3, :] + norms[0, 3:4, :]).astype(BF)


def attention_forward(layer, parts, norms, qkv_w, out_w, first):
    total, width = parts[0].shape
    images = total // PAD
    wide = qkv_w.shape[2]
    tok = lambda n: pl.BlockSpec((PAD, n), lambda i: (i, 0))
    shapes = [
        sds((total, width), BF),
        sds((total, wide), BF),
        sds((total, width), BF),
        sds((total, 128), F32),
        sds((total, width), F32),
        sds((total, width), BF),
    ]
    if not first:
        shapes.append(sds((total, width), F32))
    flops = 2 * total * width * (wide + width) + 8 * total * PAD * width
    return pl.pallas_call(
        functools.partial(attention_forward_kernel, first, len(parts)),
        grid=(images,),
        in_specs=[tok(width) for _ in parts]
        + [
            pl.BlockSpec((1, 8, width), lambda i: (layer, 0, 0)),
            pl.BlockSpec((1, width, wide), lambda i: (layer, 0, 0)),
            pl.BlockSpec((1, width, width), lambda i: (layer, 0, 0)),
        ],
        out_specs=[tok(s.shape[1]) for s in shapes],
        out_shape=shapes,
        compiler_params=params(),
        cost_estimate=cost(3 * flops, 3 * total * width * 20),
        name=f"attn_fwd_{layer}",
    )(*parts, norms, qkv_w, out_w)


def attention_backward_kernel(experts, sums, *refs):
    back = refs[:sums]
    (
        grad_r,
        input_r,
        normed_r,
        qkv_r,
        att_r,
        lse_r,
        middle_r,
        second_r,
        norms,
        router,
        counts,
        qkv_w,
        out_w,
    ) = refs[sums : sums + 13]
    grad_o, low_o, cat_o, small_o = refs[sums + 13 :]
    step = pl.program_id(0)
    width = grad_r.shape[1]
    arrived = back[0][...].astype(F32)
    for ref in back[1:]:
        arrived = arrived + ref[...].astype(F32)
    d_gates = arrived[SIDE : SIDE + 8, :PAD]
    arrived = jnp.where(iota(arrived.shape, 0) < SEQ, arrived, 0.0)
    second = second_r[...]
    probs = router_rows(router[0], second, experts)
    d_probs = d_gates + counts[0, :, 0:1]
    d_logits = probs * (d_probs - jnp.sum(probs * d_probs, axis=0, keepdims=True))
    d_logits = jnp.where(iota(d_logits.shape, 1) < SEQ, d_logits, 0.0)
    high = d_logits.astype(BF)
    low = (d_logits - high.astype(F32)).astype(BF)
    router_grad = dot(high, second) + dot(low, second)
    d_second = arrived + dot(high, router[0], TN) + dot(low, router[0], TN)

    gradient = grad_r[...].astype(F32)
    rows, scale = row_stats(middle_r[...])
    gain_second = jnp.sum(d_second * rows, axis=0, keepdims=True)
    bias_second = jnp.sum(d_second, axis=0, keepdims=True)
    d_middle = gradient + norm_back(d_second, norms[0, 2:3, :], rows, scale)
    d_branch = d_middle.astype(BF)
    cat_o[:, 3 * width :] = d_branch
    d_att = dot(d_branch, out_w[0], NT).astype(BF)
    keys_ok = iota((PAD, PAD), 1) < SEQ
    score_scale = HEAD_DIM ** (-0.5)
    for pair in range(width // 128):
        cols = slice(pair * 128, pair * 128 + 128)
        query = qkv_r[:, cols]
        key = qkv_r[:, width + pair * 128 : width + pair * 128 + 128]
        value = qkv_r[:, 2 * width + pair * 128 : 2 * width + pair * 128 + 128]
        d_pair = d_att[:, cols]
        d_q = jnp.zeros((PAD, 128), F32)
        d_k = jnp.zeros((PAD, 128), F32)
        d_v = jnp.zeros((PAD, 128), F32)
        for side, (q_h, k_h, o_h) in enumerate(
            zip(halves(query), halves(key), halves(d_pair))
        ):
            head = 2 * pair + side
            scores = dot(q_h, key, NT) * score_scale
            weights = jnp.where(keys_ok, jnp.exp(scores - lse_r[:, head : head + 1]), 0.0)
            d_v = d_v + dot(weights.astype(BF), o_h, TN)
            d_w = dot(o_h, value, NT)
            inner = jnp.sum(weights * d_w, axis=1, keepdims=True)
            d_s = (weights * (d_w - inner)).astype(BF)
            d_q = d_q + dot(d_s, k_h)
            d_k = d_k + dot(d_s, q_h, TN)
        cat_o[:, cols] = (score_scale * d_q).astype(BF)
        cat_o[:, width + pair * 128 : width + pair * 128 + 128] = (score_scale * d_k).astype(BF)
        cat_o[:, 2 * width + pair * 128 : 2 * width + pair * 128 + 128] = d_v.astype(BF)
    d_first = dot(cat_o[:, : 3 * width], qkv_w[0], NT)
    rows, scale = row_stats(input_r[...].astype(F32))
    gain_first = jnp.sum(d_first * rows, axis=0, keepdims=True)
    bias_first = jnp.sum(d_first, axis=0, keepdims=True)
    result = d_middle + norm_back(d_first, norms[0, 0:1, :], rows, scale)
    grad_o[...] = result
    low_o[...] = result.astype(BF)
    keep_old = jnp.where(step == 0, 0.0, 1.0)

    @pl.when(step == 0)
    def _():
        small_o[...] = jnp.zeros_like(small_o)

    del keep_old
    small_o[0:1, :] += gain_first
    small_o[1:2, :] += bias_first
    small_o[2:3, :] += gain_second
    small_o[3:4, :] += bias_second
    small_o[8:16, :] += router_grad


def attention_backward(
    layer, back, grad, layer_input, saved, norms, router, counts, qkv_w, out_w, experts
):
    normed, qkv, attended, lse, middle, second = saved
    total, width = grad.shape
    images = total // PAD
    wide = qkv_w.shape[2]
    tok = lambda n: pl.BlockSpec((PAD, n), lambda i: (i, 0))
    arrays = [grad, layer_input, normed, qkv, attended, lse, middle, second]
    flops = 2 * total * width * (wide + width) + 20 * total * PAD * width
    return pl.pallas_call(
        functools.partial(attention_backward_kernel, experts, len(back)),
        grid=(images,),
        in_specs=[tok(width) for _ in back]
        + [tok(a.shape[1]) for a in arrays]
        + [
            pl.BlockSpec((1, 8, width), lambda i: (layer, 0, 0)),
            pl.BlockSpec((1, 8, width), lambda i: (layer, 0, 0)),
            pl.BlockSpec((1, 8, 128), lambda i: (layer, 0, 0)),
            pl.BlockSpec((1, width, wide), lambda i: (layer, 0, 0)),
            pl.BlockSpec((1, width, width), lambda i: (layer, 0, 0)),
        ],
        out_specs=[tok(width), tok(width), tok(wide + width), whole((16, width))],
        out_shape=[
            sds((total, width), F32),
            sds((total, width), BF),
            sds((total, wide + width), BF),
            sds((16, width), F32),
        ],
        compiler_params=params(),
        cost_estimate=cost(4 * flops, 3 * total * width * 20),
        name=f"attn_bwd_{layer}",
    )(*back, *arrays, norms, router, counts, qkv_w, out_w)


def units_of(experts, images):
    return [(block, image) for block in range(experts) for image in range(images)]


def gelu_parts(pre):
    cdf = 0.5 * (1.0 + lax.erf(pre * 0.7071067811865476))
    return cdf


def expert_forward_kernel(experts, images, slot, scalars, *refs):
    tokens = refs[:experts]
    router, pos_row, pos_col, up, down = refs[experts : experts + 5]
    own_o, other_o, rows_o, gate_o, pre_o, prob_o = refs[experts + 5 : experts + 11]
    acc, back, gates = refs[experts + 11 :]
    step = pl.program_id(0)
    last = pl.num_programs(0) - 1
    me = scalars[0]
    tiles = (scalars[1 + slot] + TILE - 1) // TILE
    width = acc.shape[1]
    units = units_of(experts, images)

    @pl.when(step == 0)
    def _():
        sums = jnp.zeros((8, 128), F32)
        for u, (block, image) in enumerate(units):
            probs = router_rows(
                router[0], tokens[block][image * PAD : (image + 1) * PAD, :], experts
            )
            mine = jnp.sum(
                jnp.where(iota(probs.shape, 0) == me, probs, 0.0), axis=0, keepdims=True
            )
            gates[u : u + 1, :] = mine
            if block == 0:
                valid = jnp.where(iota(probs.shape, 1) < SEQ, probs, 0.0)
                sums = sums + jnp.sum(valid, axis=1, keepdims=True)
        prob_o[...] = sums

        @pl.loop(0, tiles)
        def _(i):
            base = i * TILE
            place = base + iota((TILE, PAD), 0)
            rows = jnp.zeros((TILE, width), F32)
            gate = jnp.zeros((TILE, 1), F32)
            for u, (block, image) in enumerate(units):
                hit = pos_row[u : u + 1, :] == place
                rows = rows + dot(
                    jnp.where(hit, 1.0, 0.0).astype(BF),
                    tokens[block][image * PAD : (image + 1) * PAD, :],
                )
                gate = gate + jnp.sum(
                    jnp.where(hit, gates[u : u + 1, :], 0.0), axis=1, keepdims=True
                )
            rows_o[pl.ds(pl.multiple_of(base, TILE), TILE), :] = rows.astype(BF)
            gate_o[pl.ds(pl.multiple_of(base, TILE), TILE), :] = gate

    @pl.loop(0, tiles)
    def _(i):
        here = pl.ds(pl.multiple_of(i * TILE, TILE), TILE)
        pre = dot(rows_o[here, :], up[0, 0])
        pre_o[here, :] = pre.astype(BF)
        hidden = (pre * gelu_parts(pre)).astype(BF)
        part = dot(hidden, down[0, 0])

        @pl.when(step == 0)
        def _():
            acc[here, :] = part

        @pl.when(step > 0)
        def _():
            acc[here, :] += part

    @pl.when(step == last)
    def _():
        scatter_rows(experts, images, slot, tiles, pos_col, acc, gate_o, back)
        per_block = images * PAD
        for block in range(experts):
            ref = own_o if block % 2 == 0 else other_o
            ref[block // 2, :, :] = back[block * per_block : (block + 1) * per_block, :].astype(
                BF
            )


def scatter_rows(experts, images, slot, tiles, pos_col, acc, gate_ref, back):
    units = units_of(experts, images)
    back[...] = jnp.zeros_like(back)

    @pl.loop(0, tiles)
    def _(i):
        here = pl.ds(pl.multiple_of(i * TILE, TILE), TILE)
        rows = acc[here, :]
        if gate_ref is not None:
            rows = rows * gate_ref[here, :]
        rows = rows.astype(BF)
        place = i * TILE + iota((PAD, TILE), 1)
        for u in range(len(units)):
            spot = slice(u * PAD, (u + 1) * PAD)
            hit = pos_col[spot, 0:1] == place
            back[spot, :] += dot(jnp.where(hit, 1.0, 0.0).astype(BF), rows)


def expert_sizes(experts, images, capacity):
    most = min(experts * images * SEQ, experts * capacity)
    return -(-most // TILE) * TILE


def expert_forward(layer, slot, scalars, blocks, router, pos_row, pos_col, up, down, capacity):
    experts = len(blocks)
    per_block, width = blocks[0].shape
    images = per_block // PAD
    hid = up.shape[3]
    step = hid // 4
    rows = expert_sizes(experts, images, capacity)
    flops = 4 * rows * width * hid // 2
    outs = [
        sds((experts // 2, per_block, width), BF),
        sds((experts // 2, per_block, width), BF),
        sds((rows, width), BF),
        sds((rows, 1), F32),
        sds((rows, hid), BF),
        sds((8, 128), F32),
    ]
    fix = lambda shape: pl.BlockSpec(shape, lambda i, s: (0,) * len(shape))
    return pl.pallas_call(
        functools.partial(expert_forward_kernel, experts, images, slot),
        grid_spec=pltpu.PrefetchScalarGridSpec(
            num_scalar_prefetch=1,
            grid=(hid // step,),
            in_specs=[fix((per_block, width)) for _ in blocks]
            + [
                pl.BlockSpec((1, 8, width), lambda i, s: (layer, 0, 0)),
                fix(pos_row.shape),
                fix(pos_col.shape),
                pl.BlockSpec((1, 1, width, step), lambda i, s: (layer, 0, 0, i)),
                pl.BlockSpec((1, 1, step, width), lambda i, s: (layer, 0, i, 0)),
            ],
            out_specs=[fix(o.shape) for o in outs[:4]]
            + [pl.BlockSpec((rows, step), lambda i, s: (0, i)), fix((8, 128))],
            scratch_shapes=[
                pltpu.VMEM((rows, width), F32),
                pltpu.VMEM((experts * per_block, width), F32),
                pltpu.VMEM((-(-experts * images // 8) * 8, PAD), F32),
            ],
        ),
        out_shape=outs,
        compiler_params=params(),
        cost_estimate=cost(2 * flops, 4 * width * hid + 2 * rows * hid),
        name=f"expert_fwd_{layer}",
    )(scalars, *blocks, router, pos_row, pos_col, up, down)


def expert_backward_kernel(experts, images, slot, scalars, *refs):
    grads = refs[:experts]
    pos_row, pos_col, gate_r, pre_r, up, down = refs[experts : experts + 6]
    own_o, other_o, dy_o, hidden_o, dpre_o = refs[experts + 6 : experts + 11]
    raw, acc, d_gate, back = refs[experts + 11 :]
    step = pl.program_id(0)
    last = pl.num_programs(0) - 1
    me = scalars[0]
    tiles = (scalars[1 + slot] + TILE - 1) // TILE
    width = acc.shape[1]
    units = units_of(experts, images)

    @pl.when(step == 0)
    def _():
        @pl.loop(0, tiles)
        def _(i):
            base = i * TILE
            here = pl.ds(pl.multiple_of(base, TILE), TILE)
            place = base + iota((TILE, PAD), 0)
            rows = jnp.zeros((TILE, width), F32)
            for u, (block, image) in enumerate(units):
                hit = pos_row[u : u + 1, :] == place
                rows = rows + dot(
                    jnp.where(hit, 1.0, 0.0).astype(BF),
                    grads[block][image * PAD : (image + 1) * PAD, :],
                )
            raw[here, :] = rows.astype(BF)
            dy_o[here, :] = (rows * gate_r[here, :]).astype(BF)

    @pl.loop(0, tiles)
    def _(i):
        here = pl.ds(pl.multiple_of(i * TILE, TILE), TILE)
        d_hidden = dot(raw[here, :], down[0, 0], NT)
        pre = pre_r[here, :].astype(F32)
        cdf = gelu_parts(pre)
        hidden = pre * cdf
        hidden_o[here, :] = hidden.astype(BF)
        gate_part = jnp.sum(hidden * d_hidden, axis=1, keepdims=True)
        slope = cdf + pre * (jnp.exp(-0.5 * pre * pre) * 0.3989422804014327)
        d_pre = (d_hidden * gate_r[here, :] * slope).astype(BF)
        dpre_o[here, :] = d_pre
        part = dot(d_pre, up[0, 0], NT)

        @pl.when(step == 0)
        def _():
            acc[here, :] = part
            d_gate[here, :] = gate_part

        @pl.when(step > 0)
        def _():
            acc[here, :] += part
            d_gate[here, :] += gate_part

    @pl.when(step == last)
    def _():
        scatter_rows(experts, images, slot, tiles, pos_col, acc, None, back)
        side = iota((8, PAD), 0)
        for u in range(len(units)):

            def gather_gate(i, total):
                here = pl.ds(pl.multiple_of(i * TILE, TILE), TILE)
                hit = pos_row[u : u + 1, :] == i * TILE + iota((TILE, PAD), 0)
                return total + jnp.sum(
                    jnp.where(hit, d_gate[here, :], 0.0), axis=0, keepdims=True
                )

            found = lax.fori_loop(0, tiles, gather_gate, jnp.zeros((1, PAD), F32))
            back[u * PAD + SIDE : (u + 1) * PAD, 0:PAD] = jnp.where(side == me, found, 0.0)
        per_block = images * PAD
        for block in range(experts):
            ref = own_o if block % 2 == 0 else other_o
            ref[block // 2, :, :] = back[block * per_block : (block + 1) * per_block, :].astype(
                BF
            )


def expert_backward(layer, slot, scalars, blocks, pos_row, pos_col, gate, pre, up, down):
    experts = len(blocks)
    per_block, width = blocks[0].shape
    images = per_block // PAD
    hid = up.shape[3]
    step = hid // 4
    rows = pre.shape[0]
    flops = 4 * rows * width * hid // 2
    outs = [
        sds((experts // 2, per_block, width), BF),
        sds((experts // 2, per_block, width), BF),
        sds((rows, width), BF),
        sds((rows, hid), BF),
        sds((rows, hid), BF),
    ]
    fix = lambda shape: pl.BlockSpec(shape, lambda i, s: (0,) * len(shape))
    cols = lambda: pl.BlockSpec((rows, step), lambda i, s: (0, i))
    return pl.pallas_call(
        functools.partial(expert_backward_kernel, experts, images, slot),
        grid_spec=pltpu.PrefetchScalarGridSpec(
            num_scalar_prefetch=1,
            grid=(hid // step,),
            in_specs=[fix((per_block, width)) for _ in blocks]
            + [
                fix(pos_row.shape),
                fix(pos_col.shape),
                fix(gate.shape),
                cols(),
                pl.BlockSpec((1, 1, width, step), lambda i, s: (layer, 0, 0, i)),
                pl.BlockSpec((1, 1, step, width), lambda i, s: (layer, 0, i, 0)),
            ],
            out_specs=[fix(o.shape) for o in outs[:3]] + [cols(), cols()],
            scratch_shapes=[
                pltpu.VMEM((rows, width), BF),
                pltpu.VMEM((rows, width), F32),
                pltpu.VMEM((rows, 1), F32),
                pltpu.VMEM((experts * per_block, width), F32),
            ],
        ),
        out_shape=outs,
        compiler_params=params(),
        cost_estimate=cost(3 * flops, 4 * width * hid + 6 * rows * hid),
        name=f"expert_bwd_{layer}",
    )(scalars, *blocks, pos_row, pos_col, gate, pre, up, down)


def expert_weights_kernel(slots, scalars, *refs):
    n = len(slots)
    lhs, rhs = refs[:n], refs[n : 2 * n]
    out = refs[2 * n]
    acc = refs[2 * n + 1]
    turned = refs[2 * n + 2 :]
    step = pl.program_id(0)
    counts = [(scalars[1 + slot] + TILE - 1) // TILE for slot in slots]

    @pl.when(step == 0)
    def _():
        for tiles, src, dst in zip(counts, lhs, turned):

            @pl.loop(0, tiles)
            def _(i):
                here = pl.ds(pl.multiple_of(i * TILE, TILE), TILE)
                dst[:, here] = src[here, :].T

    acc[...] = jnp.zeros_like(acc)
    for tiles, src, right in zip(counts, turned, rhs):

        @pl.loop(0, tiles)
        def _(i):
            here = pl.ds(pl.multiple_of(i * TILE, TILE), TILE)
            acc[...] += dot(src[:, here], right[here, :])

    out[...] = acc[...].astype(BF).reshape(out.shape)


def expert_weights(slots, scalars, lhs, rhs, blocked, parts, name):
    width = lhs[0].shape[1]
    hid = rhs[0].shape[1]
    step = hid // parts if blocked else hid // 8
    fix = lambda shape: pl.BlockSpec(shape, lambda i, s: (0,) * len(shape))
    if blocked:
        out_shape = sds((parts, width, step), BF)
        out_spec = pl.BlockSpec((1, width, step), lambda i, s: (i, 0, 0))
    else:
        out_shape = sds((width, hid), BF)
        out_spec = pl.BlockSpec((width, step), lambda i, s: (0, i))
    flops = sum(a.shape[0] for a in lhs) * width * hid
    return pl.pallas_call(
        functools.partial(expert_weights_kernel, slots),
        grid_spec=pltpu.PrefetchScalarGridSpec(
            num_scalar_prefetch=1,
            grid=(hid // step,),
            in_specs=[fix(a.shape) for a in lhs]
            + [pl.BlockSpec((a.shape[0], step), lambda i, s: (0, i)) for a in rhs],
            out_specs=out_spec,
            scratch_shapes=[pltpu.VMEM((width, step), F32)]
            + [pltpu.VMEM((width, a.shape[0]), BF) for a in lhs],
        ),
        out_shape=out_shape,
        compiler_params=params(),
        cost_estimate=cost(flops, sum(a.shape[0] for a in rhs) * hid * 2),
        name=name,
    )(scalars, *lhs, *rhs)


def dense_weights_kernel(n, *refs):
    normed, attended, right = refs[:n], refs[n : 2 * n], refs[2 * n : 3 * n]
    out = refs[3 * n]
    step = pl.program_id(0)
    last = pl.num_programs(0) - 1

    @pl.when(step < last)
    def _():
        total = dot(normed[0][...], right[0][...], TN)
        for a, b in zip(normed[1:], right[1:]):
            total = total + dot(a[...], b[...], TN)
        out[...] = total.astype(BF)

    @pl.when(step == last)
    def _():
        total = dot(attended[0][...], right[0][...], TN)
        for a, b in zip(attended[1:], right[1:]):
            total = total + dot(a[...], b[...], TN)
        out[...] = total.astype(BF)


def dense_weights(normed, attended, right, name):
    width = normed[0].shape[1]
    wide = right[0].shape[1]
    n = len(normed)
    flops = 2 * sum(a.shape[0] for a in normed) * width * wide
    return pl.pallas_call(
        functools.partial(dense_weights_kernel, n),
        grid=(wide // width,),
        in_specs=[whole(a.shape) for a in normed + attended]
        + [pl.BlockSpec((a.shape[0], width), lambda i: (0, i)) for a in right],
        out_specs=pl.BlockSpec((width, width), lambda i: (0, i)),
        out_shape=sds((width, wide), BF),
        compiler_params=params(),
        cost_estimate=cost(flops, 3 * width * wide),
        name=name,
    )(*normed, *attended, *right)


def core_swap(value):
    size = lax.axis_size("expert")
    return lax.ppermute(value, "expert", [(i, i ^ 1) for i in range(size)])


def chip_shift(value, by):
    size = lax.axis_size("expert")
    return lax.ppermute(value, "expert", [(i, (i + 2 * by) % size) for i in range(size)])


def dispatch(value):
    blocks = []
    for by in range(lax.axis_size("expert") // 2):
        own = value if by == 0 else chip_shift(value, by)
        blocks += [own, core_swap(own)]
    return blocks


def give_back(own, other):
    arrived = core_swap(other)
    parts = [own[0], arrived[0]]
    for by in range(1, own.shape[0]):
        parts.append(chip_shift(own[by] + arrived[by], -by))
    return parts


def small_sum(value):
    for axis in ("expert", "dp"):
        size, hop = lax.axis_size(axis), 1
        while hop < size:
            value = value + lax.ppermute(value, axis, [(i, i ^ hop) for i in range(size)])
            hop *= 2
    return value


def ring_order(size):
    side = 1
    while side * side * 4 <= size:
        side *= 2
    depth = size // side
    order = [z * side for z in range(depth)]
    for turn, z in enumerate(reversed(range(depth))):
        row = list(range(1, side))
        order += [z * side + x for x in (row if turn % 2 == 0 else row[::-1])]
    return order


def ring_scatter(pick):
    size = lax.axis_size("dp")
    order = ring_order(size)
    spot = [0] * size
    for place, index in enumerate(order):
        spot[index] = place
    me = jnp.asarray(spot, jnp.int32)[lax.axis_index("dp")]
    names = jnp.asarray(order, jnp.int32)
    ahead = [(order[i], order[(i + 1) % size]) for i in range(size)]
    behind = [(b, a) for a, b in ahead]

    def owner(distance):
        return names[(me + distance) % size]

    up_hops = size // 2
    down_hops = size - 1 - up_hops
    forward = backward = None
    for hop in range(up_hops):
        own = pick(owner(up_hops - hop))
        send = own if forward is None else own + forward
        forward = lax.ppermute(send, "dp", ahead)
        if hop < down_hops:
            own = pick(owner(hop - down_hops))
            send = own if backward is None else own + backward
            backward = lax.ppermute(send, "dp", behind)
    total = pick(owner(0)).astype(F32) + forward.astype(F32)
    if backward is not None:
        total = total + backward.astype(F32)
    return total


def reduce_dense(value):
    dp, experts = lax.axis_size("dp"), lax.axis_size("expert")
    rows, wide = value.shape
    piece = rows // dp // experts
    value = value.reshape(dp, experts, piece, wide)
    place = lax.axis_index("expert")
    chips = experts // 2
    parts = value.reshape(dp, chips, 2, piece, wide)
    core = place % 2
    mine = lax.dynamic_index_in_dim(parts, core, 2, keepdims=False)
    theirs = lax.dynamic_index_in_dim(parts, 1 - core, 2, keepdims=False)
    half = mine + core_swap(theirs)
    chip = place // 2
    total = lax.dynamic_index_in_dim(half, chip, 1, keepdims=False)
    for by in range(1, chips):
        out = lax.dynamic_index_in_dim(half, (chip + by) % chips, 1, keepdims=False)
        total = total + chip_shift(out, by)
    mine = ring_scatter(lambda who: lax.dynamic_index_in_dim(total, who, 0, keepdims=False))
    mine = mine.astype(BF)
    found = [mine] + [chip_shift(mine, by) for by in range(1, chips)]
    stack = jnp.stack(found)
    other = core_swap(stack)
    result = jnp.zeros((chips, 2, piece, wide), BF)
    ordered = []
    for c in range(chips):
        pick = (chip - c) % chips
        a = lax.dynamic_index_in_dim(stack, pick, 0, keepdims=False)
        b = lax.dynamic_index_in_dim(other, pick, 0, keepdims=False)
        ordered.append(jnp.where(core == 0, jnp.stack([a, b]), jnp.stack([b, a])))
    del result
    return jnp.stack(ordered).reshape(rows // dp, wide).astype(F32)


def pad_images(value):
    features = value.shape[-1]
    shaped = value.reshape(-1, SEQ, features)
    return jnp.pad(shaped, ((0, 0), (0, PAD - SEQ), (0, 0)))


def local(
    inputs,
    cotangent,
    routes,
    keep,
    norm_gain,
    norm_bias,
    qkv_weight,
    out_weight,
    router_weight,
    up_weight,
    down_weight,
):
    row_count, features = inputs.shape
    images = row_count // SEQ
    experts = lax.axis_size("expert")
    dp = lax.axis_size("dp")
    token_total = row_count * experts * dp
    capacity = 10 * row_count // (4 * experts)
    layers = qkv_weight.shape[0]
    loss_scale = 2.0 * token_total * token_total
    chunks = CHUNKS if sum(CHUNKS) == images else (1,) * images
    starts = [sum(chunks[:i]) for i in range(len(chunks))]
    n_chunks = len(chunks)
    me = lax.axis_index("expert")

    named = routes[..., None] == jnp.arange(experts, dtype=jnp.int32)
    kept = jnp.logical_and(named, keep[..., None] == 1)
    bits = jnp.sum(
        kept.astype(jnp.int32) * (1 << jnp.arange(experts, dtype=jnp.int32)), axis=(2, 3)
    )
    bits = jnp.pad(bits.reshape(layers, images, SEQ), ((0, 0), (0, 0), (0, PAD - SEQ)))
    local_counts = jnp.sum(kept.astype(F32), axis=(1, 2))
    counts = small_sum(jnp.pad(local_counts, ((0, 8 - layers), (0, 128 - experts))))
    counts = counts[:layers, :8]
    count_rows = jnp.broadcast_to(
        (BALANCE_WEIGHT * experts / loss_scale) * counts[:, :, None], (layers, 8, 128)
    )

    all_bits = dispatch(bits)
    scalars = [me.astype(jnp.int32)]
    pos_rows, pos_cols = {}, {}
    for depth in range(layers):
        for c in range(n_chunks):
            mine = jnp.stack(
                [b[depth, starts[c] : starts[c] + chunks[c]] for b in all_bits]
            )
            hit = ((mine >> me) & 1).reshape(-1)
            size = hit.shape[0]
            before = jnp.arange(size)[:, None] < jnp.arange(size)[None, :]
            ahead = jnp.dot(
                hit.astype(BF)[None, :], before.astype(BF), preferred_element_type=F32
            )[0].astype(jnp.int32)
            pos = jnp.where(hit == 1, ahead, -1)
            units = experts * chunks[c]
            row = pos.reshape(units, PAD)
            pos_rows[depth, c] = jnp.pad(
                row, ((0, -(-units // 8) * 8 - units), (0, 0)), constant_values=-1
            )
            pos_cols[depth, c] = pos.reshape(-1, 1)
            scalars.append(jnp.sum(hit).astype(jnp.int32))
    scalars = jnp.stack(scalars)

    norms = jnp.stack(
        [norm_gain[:, :, 0], norm_bias[:, :, 0], norm_gain[:, :, 1], norm_bias[:, :, 1]], axis=1
    )
    norms = jnp.pad(norms, ((0, 0), (0, 4), (0, 0)))
    router = jnp.pad(jnp.swapaxes(router_weight, 1, 2), ((0, 0), (0, 8 - experts), (0, 0)))

    padded = pad_images(inputs)
    cot_padded = pad_images(cotangent)
    cut = lambda a, c: a[starts[c] : starts[c] + chunks[c]].reshape(chunks[c] * PAD, features)
    parts = [[cut(padded, c)] for c in range(n_chunks)]
    layer_inputs, saves, expert_saves = {}, {}, {}
    prob_sums = []
    for depth in range(layers):
        moved = []
        for c in range(n_chunks):
            got = attention_forward(depth, parts[c], norms, qkv_weight, out_weight, depth == 0)
            saves[depth, c] = tuple(got[:6])
            layer_inputs[depth, c] = parts[c][0] if depth == 0 else got[6]
            moved.append(dispatch(got[5]))
        sums = jnp.zeros((8, 128), F32)
        for c in range(n_chunks):
            slot = depth * n_chunks + c
            own, other, rows, gate, pre, prob = expert_forward(
                depth,
                slot,
                scalars,
                moved[c],
                router,
                pos_rows[depth, c],
                pos_cols[depth, c],
                up_weight,
                down_weight,
                capacity,
            )
            sums = sums + prob
            expert_saves[depth, c] = (rows, gate, pre)
            parts[c] = [saves[depth, c][4]] + give_back(own, other)
        prob_sums.append(sums)

    final = [
        functools.reduce(lambda a, b: a + b, [p.astype(F32) for p in parts[c]]).astype(BF)
        for c in range(n_chunks)
    ]
    activations = jnp.concatenate(
        [f.reshape(-1, PAD, features)[:, :SEQ] for f in final]
    ).reshape(row_count, features)
    prob_total = small_sum(jnp.concatenate(prob_sums)).reshape(layers, 8, 128)[:, :, 0]
    aux_loss = jnp.sum(counts * prob_total) * (experts / loss_scale)

    grads = [cut(cot_padded, c) for c in range(n_chunks)]
    lows = grads
    small_parts, dense_out, up_out, down_out = [], [], [], []
    for depth in reversed(range(layers)):
        backs, dys, hiddens, d_pres = [], [], [], []
        for c in range(n_chunks):
            slot = depth * n_chunks + c
            blocks = dispatch(lows[c])
            rows, gate, pre = expert_saves[depth, c]
            own, other, dy, hidden, d_pre = expert_backward(
                depth,
                slot,
                scalars,
                blocks,
                pos_rows[depth, c],
                pos_cols[depth, c],
                gate,
                pre,
                up_weight,
                down_weight,
            )
            dys.append(dy)
            hiddens.append(hidden)
            d_pres.append(d_pre)
            backs.append(give_back(own, other))
        slots = [depth * n_chunks + c for c in range(n_chunks)]
        rows = [expert_saves[depth, c][0] for c in range(n_chunks)]
        lanes = up_weight.shape[3] // dp % 128 == 0
        down_g = expert_weights(slots, scalars, dys, hiddens, lanes, dp, f"down_grad_{depth}")
        if not lanes:
            down_g = down_g.reshape(features, dp, -1).swapaxes(0, 1)
        up_g = expert_weights(slots, scalars, rows, d_pres, False, dp, f"up_grad_{depth}")
        down_out.append(
            ring_scatter(lambda who: lax.dynamic_index_in_dim(down_g, who, 0, keepdims=False)).T
        )
        up_blocks = up_g.reshape(dp, -1, up_g.shape[1])
        up_out.append(
            ring_scatter(lambda who: lax.dynamic_index_in_dim(up_blocks, who, 0, keepdims=False))
        )
        smalls, cats = [], []
        for c in range(n_chunks):
            grad, low, cat, small = attention_backward(
                depth,
                backs[c],
                grads[c],
                layer_inputs[depth, c],
                saves[depth, c],
                norms,
                router,
                count_rows,
                qkv_weight,
                out_weight,
                experts,
            )
            grads[c] = grad
            if c == 0:
                lows = list(lows)
            lows[c] = low
            smalls.append(small)
            cats.append(cat)
        small_parts.append(functools.reduce(lambda a, b: a + b, smalls))
        dense = dense_weights(
            [saves[depth, c][0] for c in range(n_chunks)],
            [saves[depth, c][2] for c in range(n_chunks)],
            cats,
            f"dense_grad_{depth}",
        )
        dense_out.append(reduce_dense(dense))

    input_grad = jnp.concatenate(
        [g.reshape(-1, PAD, features)[:, :SEQ] for g in grads]
    ).reshape(row_count, features)
    small = small_sum(jnp.concatenate(small_parts)).reshape(layers, 16, features)[::-1]
    shard = features // dp
    small = lax.dynamic_slice_in_dim(small, lax.axis_index("dp") * shard, shard, 2)
    small = jnp.swapaxes(small, 1, 2)
    gain_grad = small[:, :, 0:3:2]
    bias_grad = small[:, :, 1:4:2]
    router_grad = small[:, :, 8 : 8 + experts]
    dense = jnp.stack(dense_out[::-1])
    return (
        activations,
        aux_loss,
        input_grad,
        gain_grad,
        bias_grad,
        dense[:, :, : 3 * features],
        dense[:, :, 3 * features :],
        router_grad,
        jnp.stack(up_out[::-1])[:, None],
        jnp.stack(down_out[::-1])[:, None],
    )


def solution(mesh):
    return jax.shard_map(
        local,
        mesh=mesh,
        in_specs=(
            P(("dp", "expert"), None),
            P(("dp", "expert"), None),
            P(None, ("dp", "expert"), None),
            P(None, ("dp", "expert"), None),
            P(),
            P(),
            P(),
            P(),
            P(),
            P(None, "expert", None, None),
            P(None, "expert", None, None),
        ),
        out_specs=(
            P(("dp", "expert"), None),
            P(),
            P(("dp", "expert"), None),
            P(None, "dp", None),
            P(None, "dp", None),
            P(None, "dp", None),
            P(None, "dp", None),
            P(None, "dp", None),
            P(None, "expert", "dp", None),
            P(None, "expert", "dp", None),
        ),
        check_vma=False,
    )
```
